128 devices in a mesh: sub: 32 (over z, x, core), grp: 4 (over y).
Axes of the slice: x: 4, y: 4, z: 4, core: 2. Of those that a mesh axis runs over, the one named last changes fastest.
Arguments:
- inverse_blocks: bfloat16 [32, 2048, 2048], P('sub', 'grp'), may hold values from -0.125 to 0.125
- coupling_right: bfloat16 [32, 2048, 4096], P('sub'), may hold values from -0.125 to 0.125
- coupling_left: bfloat16 [32, 32, 128, 2048], P('sub', None, None, 'grp'), may hold values from -0.0234375 to 0.0234375
- interior_rhs: bfloat16 [32, 64, 2048], P('sub'), may hold values from -6 to 6
- interface_blocks: float32 [256, 128, 128], P(('sub', 'grp')), may hold values from -0.25 to 3.25
- interface_rhs: float32 [256, 64, 128], P(('sub', 'grp')), may hold values from -6 to 6
- touched: int32 [32, 32], replicated, may hold values from 0 to 255, as said below
Outputs:
- interior_solution: bfloat16 [32, 64, 2048], P('sub', None, 'grp')
- interface_solution: float32 [256, 64, 128], P(('sub', 'grp'))
The draws below stay inside these ranges and needn't reach their ends.
Inputs may be any that keep to these rules, and one draw needn't show every extreme that they name: `touched`: entry k of a subdomain's list is a tile held by a device of grp index k // 8; the 8 entries of one grp index lie on different devices; for every grp index some device holds a tile of every subdomain's list.
All inputs are finite; a program needn't handle non-finite values.
Results may differ from the reference program's by a relative error of at most 0.013.
Values may be sent and summed in bfloat16 or wider, within the bound.
No kernel may reach another device: no remote copies, remote signals or barrier semaphores. Data moves between devices by JAX's collectives and lax.ppermute only.
A program may use at most 128 MiB of HBM per device.

```python
import jax
import jax.numpy as jnp
from jax import lax

N_INT = 2048
TILE = 128
RHS = 64
K = 32
TILES_DEV = 2
JAC = 4
SUBDOMAINS = 32
NT = 256
N_SUB = 32
N_GRP = 4


def draw_touched(key, part):
    subkeys = jax.random.split(jax.random.fold_in(key, 11), 5)
    column_tiles = K // N_GRP
    hottest = jax.random.randint(subkeys[0], (N_GRP,), 0, SUBDOMAINS)
    popularity = jax.random.randint(subkeys[1], (N_GRP, SUBDOMAINS), 0, 8)
    jitter = jax.random.randint(subkeys[2], (SUBDOMAINS, N_GRP, SUBDOMAINS), 0, 32768)
    owners = jnp.arange(SUBDOMAINS, dtype=jnp.int32)
    scores = (popularity[None, :, :] * 32768 + jitter) * 128 + owners[None, None, :]
    scores = jnp.where(owners[None, None, :] == hottest[None, :, None], 2 ** 26, scores)
    chosen = lax.top_k(scores, column_tiles)[1].astype(jnp.int32)
    order_score = jax.random.randint(subkeys[3], (SUBDOMAINS, N_GRP, column_tiles), 0, 4096) * column_tiles + jnp.arange(column_tiles, dtype=jnp.int32)
    ranking = jnp.argsort(order_score, axis=-1)
    chosen = jnp.take_along_axis(chosen, ranking, axis=-1)
    within = jax.random.randint(subkeys[4], (SUBDOMAINS, N_GRP, column_tiles), 0, TILES_DEV)
    column = jnp.arange(N_GRP, dtype=jnp.int32)[None, :, None]
    tile_ids = (chosen * N_GRP + column) * TILES_DEV + within
    return tile_ids.reshape(SUBDOMAINS, K).astype(jnp.int32)


def draw_interface_blocks(key, part):
    subkeys = jax.random.split(jax.random.fold_in(key, 23), 2)
    offdiag = jnp.clip(0.03 * jax.random.normal(subkeys[0], (NT, TILE, TILE), jnp.float32), -0.25, 0.25)
    pivots = jnp.exp(jax.random.uniform(subkeys[1], (NT, TILE), jnp.float32, 0.0, 1.0986))
    identity = jnp.eye(TILE, dtype=jnp.float32)
    return offdiag + identity[None, :, :] * pivots[:, :, None]


def shard_levels(key, dims, cuts, low, top_value):
    level, own = 1.0, jax.random.fold_in(key, 6)
    for position, parts in cuts:
        steps = jnp.exp(jax.random.uniform(jax.random.fold_in(own, position), (parts,), jnp.float32, low / len(cuts), top_value / len(cuts)))
        level = level * jnp.repeat(steps, dims[position] // parts).reshape([-1 if axis == position else 1 for axis in range(len(dims))])
    return level


def noise(own_key, dims, width, reach, shards=(), kind=jnp.bfloat16):
    gain = shard_levels(own_key, dims, shards, -0.22, 0.18) if shards else 1.0
    result = jax.random.normal(own_key, dims, jnp.float32) * width * gain
    return jnp.minimum(jnp.maximum(result, -reach), reach).astype(kind)


def setup_inputs(seed: int = 0) -> dict:
    key_list = jax.random.split(jax.random.key(seed), 8)
    inverse_blocks = noise(key_list[0], (SUBDOMAINS, N_INT, N_INT), N_INT ** -0.5, 0.125, ((0, 32), (1, 4)))
    coupling_right = noise(key_list[1], (SUBDOMAINS, N_INT, K * TILE), N_INT ** -0.5, 0.125, ((0, 32),))
    coupling_left = noise(key_list[2], (SUBDOMAINS, K, TILE, N_INT), (N_INT * N_SUB) ** -0.5, 0.0234375, ((0, 32), (3, 4)))
    interior_rhs = noise(key_list[3], (SUBDOMAINS, RHS, N_INT), 1.0, 6.0, ((0, 32),))
    interface_blocks = draw_interface_blocks(jax.random.fold_in(key_list[7], 71), 0)
    interface_rhs = noise(key_list[5], (NT, RHS, TILE), 1.0, 6.0, ((0, 128),), jnp.float32)
    touched = draw_touched(jax.random.fold_in(key_list[7], 71), 0)
    return dict(inverse_blocks=inverse_blocks, coupling_right=coupling_right, coupling_left=coupling_left, interior_rhs=interior_rhs, interface_blocks=interface_blocks, interface_rhs=interface_rhs, touched=touched)


def schur_part(packed):
    inverse, right_map, left_map, forcing = packed
    images = jnp.dot(inverse, right_map, preferred_element_type=jnp.float32).astype(jnp.bfloat16)
    images = images.reshape(N_INT, K, TILE)
    solved = jnp.dot(forcing, inverse.T, preferred_element_type=jnp.float32).astype(jnp.bfloat16)
    schur_terms = jnp.einsum("mkj,kim->kji", images.astype(jnp.float32), left_map.astype(jnp.float32))
    load_terms = jnp.einsum("cm,kim->kci", solved.astype(jnp.float32), left_map.astype(jnp.float32))
    return jnp.concatenate([schur_terms, load_terms], axis=1)


def reference(inverse_blocks, coupling_right, coupling_left, interior_rhs, interface_blocks, interface_rhs, touched):
    contributions = lax.map(schur_part, (inverse_blocks, coupling_right, coupling_left, interior_rhs))
    totals = jax.ops.segment_sum(contributions.reshape(SUBDOMAINS * K, TILE + RHS, TILE), touched.reshape(-1), num_segments=NT)
    system = jnp.swapaxes(interface_blocks, 1, 2) - totals[:, :TILE, :]
    target = interface_rhs - totals[:, TILE:, :]
    pivots = jnp.diagonal(system, axis1=1, axis2=2)
    interface_x = jnp.zeros((NT, RHS, TILE), jnp.float32)
    for sweep_no in range(JAC):
        applied = jnp.einsum("tca,taj->tcj", interface_x, system, precision=lax.Precision.HIGHEST)
        interface_x = interface_x + (target - applied) / pivots[:, None, :]
    rounded = interface_x.astype(jnp.bfloat16)

    def back_part(packed):
        inverse, right_map, forcing, row_ids = packed
        tiles_all = rounded[row_ids]
        coupled = jnp.einsum("kcj,nkj->cn", tiles_all.astype(jnp.float32), right_map.reshape(N_INT, K, TILE).astype(jnp.float32))
        remain = (forcing.astype(jnp.float32) - coupled).astype(jnp.bfloat16)
        return jnp.dot(remain, inverse.T, preferred_element_type=jnp.float32).astype(jnp.bfloat16)

    interior = lax.map(back_part, (inverse_blocks, coupling_right, interior_rhs, touched))
    return interior, interface_x
```

```python
import functools

import jax
import jax.numpy as jnp
from jax import lax
from jax.experimental import pallas as pl
from jax.experimental.pallas import tpu as pltpu
from jax.sharding import PartitionSpec as P

JAC = 4
BF = jnp.bfloat16
F32 = jnp.float32
VMEM = pl.BlockSpec(memory_space=pltpu.VMEM)
SMEM = pl.BlockSpec(memory_space=pltpu.SMEM)
HBM = pl.BlockSpec(memory_space=pl.ANY)

SIDE = 4
N_INT, QUARTER, TILE, RHS, Q = 2048, 512, 128, 64, 8
COLS = Q * TILE
HALF = (TILE + RHS) // 2


def dot(a, b, **kw):
    return jnp.dot(a, b, preferred_element_type=F32, **kw)


def dot_nt(a, b):
    return lax.dot_general(a, b, (((1,), (1,)), ((), ())), preferred_element_type=F32)


def device(sub, by_z=0, by_x=0, by_core=0):
    z, x, c = sub // 8, (sub // 2) % 4, sub % 2
    return ((z + by_z) % SIDE * SIDE + (x + by_x) % SIDE) * 2 + (c + by_core) % 2


def shift(x, **by):
    return lax.ppermute(x, "sub", [(s, device(s, **by)) for s in range(32)])


def shift_grp(x, by):
    return lax.ppermute(x, "grp", [(s, (s + by) % 4) for s in range(4)])


def call(kernel, out_shape, in_specs, name, out_specs=None, scratch=(), flops=0, nbytes=0, **kw):
    if out_specs is None:
        out_specs = jax.tree.map(lambda _: VMEM, out_shape)
    return pl.pallas_call(
        kernel,
        out_shape=out_shape,
        in_specs=in_specs,
        out_specs=out_specs,
        scratch_shapes=scratch,
        compiler_params=pltpu.CompilerParams(vmem_limit_bytes=48 << 20, **kw),
        cost_estimate=pl.CostEstimate(flops=flops, bytes_accessed=nbytes, transcendentals=0),
        name=name,
    )


def quarter_kernel(rel, first, last, *refs):
    refs = list(refs)
    inv, right, left = refs[:3]
    del refs[:3]
    if first:
        forcing = refs.pop(0)
    else:
        solved_in, cur = refs[:2]
        del refs[:2]
    tiles, images = refs[:2]
    del refs[:2]
    if first:
        solved_f, solved_b = refs[:2]
        del refs[:2]
    if not last:
        nxt = refs.pop(0)
    left_buf, sem = refs[:2]
    g = lax.axis_index("grp")
    q = lax.rem(g + rel[0], 4)
    left_copy = pltpu.make_async_copy(left.at[pl.ds(q * Q, Q)], left_buf, sem.at[0])
    if first:
        cur = refs[2]
        parts = []
        for h in range(2):
            cols = pl.ds(pl.multiple_of(q * COLS + h * 512, 512), 512)
            copy = pltpu.make_async_copy(right.at[:, cols], cur.at[:, pl.ds(h * 512, 512)], sem.at[2 + h])
            copy.start()
            parts.append(copy)
    left_copy.start()
    if not last:
        qn = lax.rem(g + rel[1], 4)
        cols = pl.ds(pl.multiple_of(qn * COLS, COLS), COLS)
        next_copy = pltpu.make_async_copy(right.at[:, cols], nxt, sem.at[1])
    if first:
        s = dot_nt(forcing[...], inv[...])
        solved_f[...] = s
        solved = s.astype(BF)
        solved_b[...] = solved
        for h in range(2):
            parts[h].wait()
            if h == 1:
                left_copy.wait()
                next_copy.start()
            images[:, h * 512 : (h + 1) * 512] = dot(inv[...], cur[:, h * 512 : (h + 1) * 512]).astype(BF)
    else:
        if not last:
            next_copy.start()
        solved = solved_in[...]
        images[...] = dot(inv[...], cur[...]).astype(BF)
        left_copy.wait()
    for t in range(Q):
        lk = left_buf[t]
        tiles[t, :TILE] = dot(lk, images[:, t * TILE : (t + 1) * TILE]).astype(BF)
        tiles[t, TILE:] = dot_nt(solved, lk).astype(BF)
    if not last:
        next_copy.wait()


def quarter_call(rel, first, last, operands):
    shape = jax.ShapeDtypeStruct
    in_specs = [VMEM, HBM, HBM] + ([VMEM] if first else [VMEM, VMEM])
    outs = [shape((Q, TILE + RHS, TILE), BF), shape((QUARTER, COLS), BF)]
    if first:
        outs += [shape((RHS, QUARTER), F32), shape((RHS, QUARTER), BF)]
    if not last:
        outs += [shape((N_INT, COLS), BF)]
    scratch = [pltpu.VMEM((Q, TILE, QUARTER), BF), pltpu.SemaphoreType.DMA((4,))]
    if first:
        scratch.append(pltpu.VMEM((N_INT, COLS), BF))
    return call(
        functools.partial(quarter_kernel, rel, first, last),
        outs,
        in_specs,
        f"quarter{rel[0]}",
        scratch=scratch,
        flops=2 * QUARTER * N_INT * COLS,
        nbytes=N_INT * COLS * 2,
    )(*operands)


def sum_kernel(own, r1, r2, r3, a, b):
    for t in range(Q):
        s = (own[t].astype(F32) + r1[t].astype(F32)) + (r2[t].astype(F32) + r3[t].astype(F32))
        a[t] = s[:HALF].astype(BF)
        b[t] = s[HALF:].astype(BF)


def position():
    sub = lax.axis_index("sub")
    return sub, lax.axis_index("grp"), sub >> 3, (sub >> 1) & 3, sub & 1


def owner(tile):
    s = tile >> 3
    return s >> 3, (s >> 1) & 3, s & 1, tile & 1


def place_kernel(touched, *refs):
    a, b = refs[:4], refs[4:8]
    mine, other, acc = refs[8:]
    sub, g, z, x, c = position()
    mine[...] = jnp.zeros_like(mine)
    acc[...] = jnp.zeros_like(acc)
    for d in range(SIDE):
        from_a = (z << 3) | (((x - d) & 3) << 1) | c
        from_b = (((z - d) & 3) << 3) | (x << 1) | c

        @pl.loop(0, Q)
        def _(q):
            oz, ox, oc, t = owner(touched[from_a, g * Q + q])
            slot = ((oz - z) & 3) * 2 + t

            @pl.when((ox == x) & (oc == c))
            def _():
                mine[0, slot] += a[d][q].astype(F32)

            @pl.when((ox == x) & (oc != c))
            def _():
                acc[0, slot] += a[d][q].astype(F32)

            oz, ox, oc, t = owner(touched[from_b, g * Q + q])
            slot_b = ((ox - x) & 3) * 2 + t

            @pl.when((oz == z) & (oc == c))
            def _():
                mine[1, slot_b] += b[d][q].astype(F32)

            @pl.when((oz == z) & (oc != c))
            def _():
                acc[1, slot_b] += b[d][q].astype(F32)

    other[...] = acc[...].astype(BF)


def fold_kernel(mine, arrived, own, *outs):
    for h in range(2):
        for d in range(SIDE):
            s = mine[h, 2 * d : 2 * d + 2] + arrived[h, 2 * d : 2 * d + 2].astype(F32)
            if d == 0:
                own[h] = s
            else:
                outs[3 * h + d - 1][...] = s.astype(BF)


def solve_kernel(own, a1, a2, a3, b1, b2, b3, blocks, rhs, x_out, xa, xb, sys_t):
    row = lax.broadcasted_iota(jnp.int32, (TILE, TILE), 0)
    col = lax.broadcasted_iota(jnp.int32, (TILE, TILE), 1)
    cut = TILE - HALF
    for t in range(2):
        total_a = own[0, t] + a1[t].astype(F32) + a2[t].astype(F32) + a3[t].astype(F32)
        total_b = own[1, t] + b1[t].astype(F32) + b2[t].astype(F32) + b3[t].astype(F32)
        sys_t[t, :HALF] = blocks[t, :HALF] - total_a
        sys_t[t, HALF:] = blocks[t, HALF:] - total_b[:cut]
        m = sys_t[t]
        system = m.T
        target = rhs[t] - total_b[cut:]
        pivots = jnp.sum(jnp.where(row == col, m, 0.0), axis=0, keepdims=True)
        x = target / pivots
        for _ in range(JAC - 1):
            x = x + (target - dot(x, system, precision=lax.Precision.HIGHEST)) / pivots
        x_out[t] = x
        r = x.astype(BF)
        xa[t] = r[: RHS // 2]
        xb[t] = r[RHS // 2 :]


def stack_kernel(*refs):
    for h in range(2):
        for d in range(SIDE):
            refs[8 + h][d] = refs[4 * h + d][...]


def pick_kernel(touched, *refs):
    a, b = refs[:4], refs[4:8]
    mine, other = refs[8:]
    sub, g, z, x, c = position()
    mine[...] = jnp.zeros_like(mine)
    other[...] = jnp.zeros_like(other)
    half = RHS // 2
    for reader, out in ((sub, mine), (sub ^ 1, other)):

        @pl.loop(0, Q)
        def _(q):
            oz, ox, oc, t = owner(touched[reader, g * Q + q])
            dz, dx = (z - oz) & 3, (x - ox) & 3
            for e in range(SIDE):

                @pl.when((oc == c) & (dz == e))
                def _():
                    out[q, :half] = a[e][dx, t]

                @pl.when((oc == c) & (dx == e))
                def _():
                    out[q, half:] = b[e][dz, t]


def final_kernel(x0, x1, x2, x3, i0, i1, i2, i3, solved, out, wide):
    acc = solved[...]
    for xr, im in ((x0, i0), (x1, i3), (x2, i2), (x3, i1)):
        for q in range(Q):
            wide[:, q * TILE : (q + 1) * TILE] = xr[q]
        acc = acc - dot_nt(wide[...], im[...])
    out[...] = acc.astype(BF)


def shards(
    inverse_blocks,
    coupling_right,
    coupling_left,
    interior_rhs,
    interface_blocks,
    interface_rhs,
    touched,
):
    shape = jax.ShapeDtypeStruct
    inverse, right, left, forcing = inverse_blocks[0], coupling_right[0], coupling_left[0], interior_rhs[0]

    t2, im2, solved_f, solved_b, nxt = quarter_call((2, 1), True, False, (inverse, right, left, forcing))
    r2 = shift_grp(t2, 2)
    t1, im1, nxt = quarter_call((1, 3), False, False, (inverse, right, left, solved_b, nxt))
    r1 = shift_grp(t1, 1)
    t3, im3, nxt = quarter_call((3, 0), False, False, (inverse, right, left, solved_b, nxt))
    r3 = shift_grp(t3, 3)
    t0, im0 = quarter_call((0, 0), False, True, (inverse, right, left, solved_b, nxt))

    half = shape((Q, HALF, TILE), BF)
    a, b = call(sum_kernel, [half, half], [VMEM] * 4, "grp_sum")(t0, r1, r2, r3)
    along_x = [a] + [shift(a, by_x=d) for d in (1, 2, 3)]
    along_z = [b] + [shift(b, by_z=d) for d in (1, 2, 3)]
    slots = (2, 2 * SIDE, HALF, TILE)
    mine, other = call(
        place_kernel,
        [shape(slots, F32), shape(slots, BF)],
        [SMEM] + [VMEM] * 8,
        "place",
        scratch=[pltpu.VMEM(slots, F32)],
    )(touched, *along_x, *along_z)
    arrived = shift(other, by_core=1)
    piece = shape((2, HALF, TILE), BF)
    own, a1, a2, a3, b1, b2, b3 = call(
        fold_kernel, [shape((2, 2, HALF, TILE), F32)] + [piece] * 6, [VMEM] * 2, "fold"
    )(mine, arrived)
    pieces = [shift(p, by_z=d) for d, p in ((1, a1), (2, a2), (3, a3))]
    pieces += [shift(p, by_x=d) for d, p in ((1, b1), (2, b2), (3, b3))]

    narrow = shape((2, RHS // 2, TILE), BF)
    x, xa, xb = call(
        solve_kernel,
        [shape((2, RHS, TILE), F32), narrow, narrow],
        [VMEM] * 9,
        "solve",
        scratch=[pltpu.VMEM((2, TILE, TILE), F32)],
    )(own, *pieces, interface_blocks, interface_rhs)

    xs = [xa] + [shift(xa, by_x=d) for d in (1, 2, 3)]
    xs += [xb] + [shift(xb, by_z=d) for d in (1, 2, 3)]
    stack = shape((SIDE, 2, RHS // 2, TILE), BF)
    pa, pb = call(stack_kernel, [stack, stack], [VMEM] * 8, "stack")(*xs)
    ya = [pa] + [shift(pa, by_z=d) for d in (1, 2, 3)]
    yb = [pb] + [shift(pb, by_x=d) for d in (1, 2, 3)]
    wanted = shape((Q, RHS, TILE), BF)
    keep, give = call(pick_kernel, [wanted, wanted], [SMEM] + [VMEM] * 8, "pick")(touched, *ya, *yb)
    x0 = keep + shift(give, by_core=1)
    x1, x2, x3 = (shift_grp(x0, d) for d in (1, 2, 3))
    interior = call(
        final_kernel,
        shape((RHS, QUARTER), BF),
        [VMEM] * 9,
        "interior",
        scratch=[pltpu.VMEM((RHS, COLS), BF)],
        flops=2 * RHS * QUARTER * COLS * 4,
        nbytes=1 << 22,
    )(x0, x1, x2, x3, im0, im1, im2, im3, solved_f)
    return (interior[None], x)


def solution(mesh):
    in_specs = (
        P("sub", "grp", None),
        P("sub", None, None),
        P("sub", None, None, "grp"),
        P("sub", None, None),
        P(("sub", "grp"), None, None),
        P(("sub", "grp"), None, None),
        P(),
    )
    out_specs = (P("sub", None, "grp"), P(("sub", "grp"), None, None))
    return jax.shard_map(shards, mesh=mesh, in_specs=in_specs, out_specs=out_specs, check_vma=False)
```

```python
import functools

import jax
import jax.numpy as jnp
from jax import lax
from jax.experimental import pallas as pl
from jax.experimental.pallas import tpu as pltpu
from jax.sharding import PartitionSpec as P

JAC = 4
BF = jnp.bfloat16
F32 = jnp.float32
VMEM = pl.BlockSpec(memory_space=pltpu.VMEM)
SMEM = pl.BlockSpec(memory_space=pltpu.SMEM)
HBM = pl.BlockSpec(memory_space=pltpu.HBM)

SUBS = 32
N_INT, QUARTER, TILE, RHS, Q = 2048, 512, 128, 64, 8
COLS = Q * TILE
ROWS = TILE + RHS
PARTS, DEPTH = 4, 512


def dot(a, b, **kw):
    return jnp.dot(a, b, preferred_element_type=F32, **kw)


def dot_nt(a, b):
    return lax.dot_general(a, b, (((1,), (1,)), ((), ())), preferred_element_type=F32)


def shift_grp(x, by):
    return lax.ppermute(x, "grp", [(s, (s + by) % 4) for s in range(4)])


def call(kernel, out_shape, in_specs, name, out_specs=None, scratch=(), flops=0, nbytes=0, mib=8):
    if out_specs is None:
        out_specs = jax.tree.map(lambda _: VMEM, out_shape)
    return pl.pallas_call(
        kernel,
        out_shape=out_shape,
        in_specs=in_specs,
        out_specs=out_specs,
        scratch_shapes=scratch,
        compiler_params=pltpu.CompilerParams(vmem_limit_bytes=mib << 20),
        cost_estimate=pl.CostEstimate(flops=flops, bytes_accessed=nbytes, transcendentals=0),
        name=name,
    )


def start_loads(rel, right, left, cur, left_buf, sem):
    q = lax.rem(lax.axis_index("grp") + rel, 4)
    cols = pl.ds(pl.multiple_of(q * COLS, COLS), COLS)
    copies = []
    for k in range(PARTS):
        rows = pl.ds(k * DEPTH, DEPTH)
        copies.append(pltpu.make_async_copy(right.at[rows, cols], cur.at[rows], sem.at[k]))
    copies.append(pltpu.make_async_copy(left.at[pl.ds(q * Q, Q)], left_buf, sem.at[PARTS]))
    for c in copies:
        c.start()
    return copies


def make_tiles(copies, inv, solved, cur, left, acc, tiles, images):
    for k in range(PARTS):
        copies[k].wait()
        rows = slice(k * DEPTH, (k + 1) * DEPTH)
        p = dot(inv[:, rows], cur[rows])
        if k == 0:
            acc[...] = p
        elif k < PARTS - 1:
            acc[...] += p
        else:
            images[...] = (acc[...] + p).astype(BF)
    copies[PARTS].wait()
    for t in range(Q):
        lk = left[t]
        tiles[t, :TILE] = dot(lk, images[:, t * TILE : (t + 1) * TILE]).astype(BF)
        tiles[t, TILE:] = dot_nt(solved, lk).astype(BF)


def first_kernel(inv_h, right, left, forcing_h, tiles, images, solved_f, solved_b, inv, forcing, cur, left_buf, acc, sem):
    early = [
        pltpu.make_async_copy(inv_h, inv, sem.at[PARTS + 1]),
        pltpu.make_async_copy(forcing_h, forcing, sem.at[PARTS + 2]),
    ]
    for c in early:
        c.start()
    copies = start_loads(2, right, left, cur, left_buf, sem)
    for c in early:
        c.wait()
    s = dot_nt(forcing[...], inv[...])
    solved_f[...] = s
    solved_b[...] = s.astype(BF)
    make_tiles(copies, inv, solved_b[...], cur, left_buf, acc, tiles, images)


def middle_kernel(rel, inv, right, left, solved, tiles, images, cur, left_buf, acc, sem):
    copies = start_loads(rel, right, left, cur, left_buf, sem)
    make_tiles(copies, inv, solved[...], cur, left_buf, acc, tiles, images)


def last_kernel(inv, right, left, solved, touched, tiles, images, reads, cur, left_buf, acc, sem):
    copies = start_loads(0, right, left, cur, left_buf, sem)
    make_tiles(copies, inv, solved[...], cur, left_buf, acc, tiles, images)
    sub, g = lax.axis_index("sub"), lax.axis_index("grp")
    first = (sub * 4 + g) * 2

    @pl.loop(0, SUBS)
    def _(s):
        found = jnp.int32(0)
        for k in range(Q):
            tile = touched[s, g * Q + k]
            found = jnp.where((tile >> 1) == (first >> 1), 1 + (tile & 1), found)
        reads[s] = found


def place_kernel(touched, own, r1, r2, r3, out):
    sub, g = lax.axis_index("sub"), lax.axis_index("grp")
    out[...] = jnp.zeros_like(out)
    for t in range(Q):
        s = (own[t].astype(F32) + r1[t].astype(F32)) + (r2[t].astype(F32) + r3[t].astype(F32))
        out[touched[sub, g * Q + t] >> 3] = s.astype(BF)


def solve_kernel(reads, arrived, blocks, rhs, x_out, out, total, rounded):
    total[...] = jnp.zeros_like(total)

    @pl.loop(0, SUBS)
    def _(s):
        which = reads[s]

        @pl.when(which > 0)
        def _():
            total[which - 1] += arrived[s].astype(F32)

    row = lax.broadcasted_iota(jnp.int32, (TILE, TILE), 0)
    col = lax.broadcasted_iota(jnp.int32, (TILE, TILE), 1)
    for t in range(2):
        m = blocks[t] - total[t, :TILE]
        system = m.T
        target = rhs[t] - total[t, TILE:]
        pivots = jnp.sum(jnp.where(row == col, m, 0.0), axis=0, keepdims=True)
        x = target / pivots
        for _ in range(JAC - 1):
            x = x + (target - dot(x, system, precision=lax.Precision.HIGHEST)) / pivots
        x_out[t] = x
        rounded[t] = x.astype(BF)

    @pl.loop(0, SUBS)
    def _(s):
        out[s] = rounded[jnp.maximum(reads[s] - 1, 0)]


def pick_kernel(touched, returned, out):
    sub, g = lax.axis_index("sub"), lax.axis_index("grp")
    for q in range(Q):
        tile = returned[touched[sub, g * Q + q] >> 3]
        for p in range(4):
            out[p, q] = tile


def final_kernel(tiles, i0, i1, i2, i3, solved, out, wide):
    g = lax.axis_index("grp")
    acc = solved[...]
    for r, im in enumerate((i0, i1, i2, i3)):
        p = lax.rem(g + r, 4)
        for q in range(Q):
            wide[:, q * TILE : (q + 1) * TILE] = tiles[p, q]
        acc = acc - dot_nt(wide[...], im[...])
    out[...] = acc.astype(BF)


def shards(
    inverse_blocks,
    coupling_right,
    coupling_left,
    interior_rhs,
    interface_blocks,
    interface_rhs,
    touched,
):
    shape = jax.ShapeDtypeStruct
    inverse, right, left, forcing = inverse_blocks[0], coupling_right[0], coupling_left[0], interior_rhs[0]
    tiles, images = shape((Q, ROWS, TILE), BF), shape((QUARTER, COLS), BF)
    scratch = [
        pltpu.VMEM((N_INT, COLS), BF),
        pltpu.VMEM((Q, TILE, QUARTER), BF),
        pltpu.VMEM((QUARTER, COLS), F32),
        pltpu.SemaphoreType.DMA((PARTS + 3,)),
    ]
    cost = dict(flops=2 * QUARTER * N_INT * COLS, nbytes=N_INT * COLS * 2, mib=50)

    t2, im2, solved_f, solved_b, inv = call(
        first_kernel,
        [tiles, images, shape((RHS, QUARTER), F32), shape((RHS, QUARTER), BF), shape((QUARTER, N_INT), BF)],
        [HBM] * 4,
        "quarter2",
        scratch=[pltpu.VMEM((RHS, N_INT), BF)] + scratch,
        **cost,
    )(inverse, right, left, forcing)
    r2 = shift_grp(t2, 2)
    t1, im1 = call(
        functools.partial(middle_kernel, 1), [tiles, images], [VMEM, HBM, HBM, VMEM], "quarter1", scratch=scratch, **cost
    )(inv, right, left, solved_b)
    r1 = shift_grp(t1, 1)
    t3, im3 = call(
        functools.partial(middle_kernel, 3), [tiles, images], [VMEM, HBM, HBM, VMEM], "quarter3", scratch=scratch, **cost
    )(inv, right, left, solved_b)
    r3 = shift_grp(t3, 3)
    t0, im0, reads = call(
        last_kernel,
        [tiles, images, shape((SUBS,), jnp.int32)],
        [VMEM, HBM, HBM, VMEM, SMEM],
        "quarter0",
        out_specs=[VMEM, VMEM, SMEM],
        scratch=scratch,
        **cost,
    )(inv, right, left, solved_b, touched)

    outgoing = call(place_kernel, shape((SUBS, ROWS, TILE), BF), [SMEM] + [VMEM] * 4, "place")(
        touched, t0, r1, r2, r3
    )
    arrived = lax.all_to_all(outgoing, "sub", 0, 0, tiled=True)
    x, leaving = call(
        solve_kernel,
        [shape((2, RHS, TILE), F32), shape((SUBS, RHS, TILE), BF)],
        [SMEM] + [VMEM] * 3,
        "solve",
        scratch=[pltpu.VMEM((2, ROWS, TILE), F32), pltpu.VMEM((2, RHS, TILE), BF)],
    )(reads, arrived, interface_blocks, interface_rhs)
    returned = lax.all_to_all(leaving, "sub", 0, 0, tiled=True)
    wanted = call(pick_kernel, shape((4, Q, RHS, TILE), BF), [SMEM, VMEM], "pick")(touched, returned)
    gathered = lax.all_to_all(wanted, "grp", 0, 0, tiled=True)
    interior = call(
        final_kernel,
        shape((RHS, QUARTER), BF),
        [VMEM] * 6,
        "interior",
        scratch=[pltpu.VMEM((RHS, COLS), BF)],
        flops=2 * RHS * QUARTER * COLS * 4,
        nbytes=1 << 22,
    )(gathered, im0, im1, im2, im3, solved_f)
    return (interior[None], x)


def solution(mesh):
    in_specs = (
        P("sub", "grp", None),
        P("sub", None, None),
        P("sub", None, None, "grp"),
        P("sub", None, None),
        P(("sub", "grp"), None, None),
        P(("sub", "grp"), None, None),
        P(),
    )
    out_specs = (P("sub", None, "grp"), P(("sub", "grp"), None, None))
    return jax.shard_map(shards, mesh=mesh, in_specs=in_specs, out_specs=out_specs, check_vma=False)
```

```python
import functools

import jax
import jax.numpy as jnp
from jax import lax
from jax.experimental import pallas as pl
from jax.experimental.pallas import tpu as pltpu
from jax.sharding import PartitionSpec as P

JAC = 4
BF = jnp.bfloat16
F32 = jnp.float32
VMEM = pl.BlockSpec(memory_space=pltpu.VMEM)
SMEM = pl.BlockSpec(memory_space=pltpu.SMEM)
HBM = pl.BlockSpec(memory_space=pltpu.HBM)

SUBS = 32
N_INT, QUARTER, TILE, RHS, Q = 2048, 512, 128, 64, 8
COLS = Q * TILE
ROWS = TILE + RHS
HALF = ROWS // 2
PARTS, DEPTH = 4, 512
STREAMS = 8


def dot(a, b, **kw):
    return jnp.dot(a, b, preferred_element_type=F32, **kw)


def dot_nt(a, b):
    return lax.dot_general(a, b, (((1,), (1,)), ((), ())), preferred_element_type=F32)


def shift_grp(x, by):
    return lax.ppermute(x, "grp", [(s, (s + by) % 4) for s in range(4)])


def call(kernel, out_shape, in_specs, name, out_specs=None, scratch=(), flops=0, nbytes=0, mib=8):
    if out_specs is None:
        out_specs = jax.tree.map(lambda _: VMEM, out_shape)
    return pl.pallas_call(
        kernel,
        out_shape=out_shape,
        in_specs=in_specs,
        out_specs=out_specs,
        scratch_shapes=scratch,
        compiler_params=pltpu.CompilerParams(vmem_limit_bytes=mib << 20),
        cost_estimate=pl.CostEstimate(flops=flops, bytes_accessed=nbytes, transcendentals=0),
        name=name,
    )


def block_copies(rel, right, left, cur, left_buf, sem):
    q = lax.rem(lax.axis_index("grp") + rel, 4)
    cols = pl.ds(pl.multiple_of(q * COLS, COLS), COLS)
    copies = []
    for k in range(STREAMS):
        rows = pl.ds(k * (N_INT // STREAMS), N_INT // STREAMS)
        copies.append(pltpu.make_async_copy(right.at[rows, cols], cur.at[rows], sem.at[k]))
    for k in range(2):
        tiles = pl.ds(k * (Q // 2), Q // 2)
        src = left.at[pl.ds(q * Q + k * (Q // 2), Q // 2)]
        copies.append(pltpu.make_async_copy(src, left_buf.at[tiles], sem.at[STREAMS + k]))
    return copies


def make_images(inv, cur, images):
    @pl.loop(0, 2)
    def _(h):
        rows = pl.ds(pl.multiple_of(h * (QUARTER // 2), QUARTER // 2), QUARTER // 2)
        images[rows, :] = dot(inv[rows, :], cur[...]).astype(BF)


def make_tiles(solved, left, images, tiles):
    load = dot_nt(solved, left[...].reshape(COLS, QUARTER))
    for t in range(Q):
        cols = slice(t * TILE, (t + 1) * TILE)
        tiles[t, :TILE] = dot(left[t], images[:, cols]).astype(BF)
        tiles[t, TILE:] = load[:, cols].astype(BF)


def first_kernel(
    inv_h, right, left, forcing_h, tiles, images, solved_f, solved_b, inv, nxt, nxt_left,
    forcing, cur, left_buf, acc, sem, part_sem,
):
    q = lax.rem(lax.axis_index("grp") + 2, 4)
    cols = pl.ds(pl.multiple_of(q * COLS, COLS), COLS)
    parts = []
    for k in range(PARTS):
        rows = pl.ds(k * DEPTH, DEPTH)
        parts.append((
            pltpu.make_async_copy(inv_h.at[:, rows], inv.at[:, rows], part_sem.at[2 * k]),
            pltpu.make_async_copy(right.at[rows, cols], cur.at[rows], part_sem.at[2 * k + 1]),
        ))
        for c in parts[-1]:
            c.start()
    late = [
        pltpu.make_async_copy(forcing_h, forcing, part_sem.at[2 * PARTS]),
        pltpu.make_async_copy(left.at[pl.ds(q * Q, Q)], left_buf, part_sem.at[2 * PARTS + 1]),
    ]
    for c in late:
        c.start()
    following = block_copies(1, right, left, nxt, nxt_left, sem)
    for k in range(PARTS):
        for c in parts[k]:
            c.wait()
        if k == PARTS - 2:
            for c in following:
                c.start()
        part = slice(k * DEPTH, (k + 1) * DEPTH)
        p = dot(inv[:, part], cur[part])
        if k == 0:
            acc[...] = p
        elif k < PARTS - 1:
            acc[...] += p
        else:
            images[...] = (acc[...] + p).astype(BF)
    for c in late:
        c.wait()
    s = dot_nt(forcing[...], inv[...])
    solved_f[...] = s
    solved_b[...] = s.astype(BF)
    make_tiles(solved_b[...], left_buf, images, tiles)
    for c in following:
        c.wait()


def middle_kernel(rel, inv, right, left, solved, cur, cur_left, tiles, images, nxt, nxt_left, sem):
    following = block_copies(rel, right, left, nxt, nxt_left, sem)
    for c in following:
        c.start()
    make_images(inv, cur, images)
    make_tiles(solved[...], cur_left, images, tiles)
    for c in following:
        c.wait()


def last_kernel(inv, solved, cur, cur_left, touched, tiles, images, reads):
    make_images(inv, cur, images)
    make_tiles(solved[...], cur_left, images, tiles)
    sub, g = lax.axis_index("sub"), lax.axis_index("grp")
    first = (sub * 4 + g) * 2

    @pl.loop(0, SUBS)
    def _(s):
        found = jnp.int32(0)
        for k in range(Q):
            tile = touched[s, g * Q + k]
            found = jnp.where((tile >> 1) == (first >> 1), 1 + (tile & 1), found)
        reads[s] = found


def place_kernel(touched, own, r1, r2, r3, out):
    sub, g = lax.axis_index("sub"), lax.axis_index("grp")
    out[...] = jnp.zeros_like(out)
    for t in range(Q):
        s = (own[t].astype(F32) + r1[t].astype(F32)) + (r2[t].astype(F32) + r3[t].astype(F32))
        out[touched[sub, g * Q + t] >> 3] = s.astype(BF)


def solve_kernel(reads, arrived, blocks, rhs, x_out, out, total, rounded):
    total[...] = jnp.zeros_like(total)

    @pl.loop(0, SUBS)
    def _(s):
        which = reads[s]

        @pl.when(which > 0)
        def _():
            total[which - 1] += arrived[s].astype(F32)

    row = lax.broadcasted_iota(jnp.int32, (TILE, TILE), 0)
    col = lax.broadcasted_iota(jnp.int32, (TILE, TILE), 1)
    systems, targets, pivots, xs = [], [], [], []
    for t in range(2):
        m = blocks[t] - total[t, :TILE]
        systems.append(m.T)
        targets.append(rhs[t] - total[t, TILE:])
        pivots.append(jnp.sum(jnp.where(row == col, m, 0.0), axis=0, keepdims=True))
        xs.append(targets[t] / pivots[t])
    for _ in range(JAC - 1):
        applied = [dot(xs[t], systems[t], precision=lax.Precision.HIGHEST) for t in range(2)]
        xs = [xs[t] + (targets[t] - applied[t]) / pivots[t] for t in range(2)]
    for t in range(2):
        x_out[t] = xs[t]
        rounded[t] = xs[t].astype(BF)

    @pl.loop(0, SUBS)
    def _(s):
        out[s] = rounded[jnp.maximum(reads[s] - 1, 0)]


def pick_kernel(touched, returned, out):
    sub, g = lax.axis_index("sub"), lax.axis_index("grp")
    for q in range(Q):
        out[q] = returned[touched[sub, g * Q + q] >> 3]


def coupled(tiles, images, wide):
    for q in range(Q):
        wide[:, q * TILE : (q + 1) * TILE] = tiles[q]
    return dot_nt(wide[...], images[...])


def own_kernel(x0, i0, solved, out, wide):
    out[...] = solved[...] - coupled(x0, i0, wide)


def final_kernel(start, i1, i2, i3, x1, x3, x2, out, *wide):
    acc = start[...]
    for xr, im, w in zip((x1, x3, x2), (i3, i1, i2), wide):
        acc = acc - coupled(xr, im, w)
    out[...] = acc.astype(BF)


def shards(
    inverse_blocks,
    coupling_right,
    coupling_left,
    interior_rhs,
    interface_blocks,
    interface_rhs,
    touched,
):
    shape = jax.ShapeDtypeStruct
    inverse, right, left, forcing = inverse_blocks[0], coupling_right[0], coupling_left[0], interior_rhs[0]
    tiles, images = shape((Q, ROWS, TILE), BF), shape((QUARTER, COLS), BF)
    block = [shape((N_INT, COLS), BF), shape((Q, TILE, QUARTER), BF)]
    dma = pltpu.SemaphoreType.DMA
    cost = dict(flops=2 * QUARTER * N_INT * COLS, nbytes=N_INT * COLS * 2, mib=20)
    inverse, right, left, forcing = (
        pltpu.with_memory_space_constraint(v, pltpu.HBM) for v in (inverse, right, left, forcing)
    )
    t2, im2, solved_f, solved_b, inv, *nxt = call(
        first_kernel,
        [tiles, images, shape((RHS, QUARTER), F32), shape((RHS, QUARTER), BF), shape((QUARTER, N_INT), BF)] + block,
        [HBM] * 4,
        "quarter2",
        scratch=[
            pltpu.VMEM((RHS, N_INT), BF),
            pltpu.VMEM((N_INT, COLS), BF),
            pltpu.VMEM((Q, TILE, QUARTER), BF),
            pltpu.VMEM((QUARTER, COLS), F32),
            dma((STREAMS + 2,)),
            dma((2 * PARTS + 2,)),
        ],
        **cost,
    )(inverse, right, left, forcing)
    r2 = shift_grp(t2, 2)
    middle = lambda rel, following: call(
        functools.partial(middle_kernel, following),
        [tiles, images] + block,
        [VMEM, HBM, HBM, VMEM, VMEM, VMEM],
        f"quarter{rel}",
        scratch=[dma((STREAMS + 2,))],
        **cost,
    )
    t1, im1, *nxt = middle(1, 3)(inv, right, left, solved_b, *nxt)
    r1 = shift_grp(t1, 1)
    t3, im3, *nxt = middle(3, 0)(inv, right, left, solved_b, *nxt)
    r3 = shift_grp(t3, 3)
    t0, im0, reads = call(
        last_kernel,
        [tiles, images, shape((SUBS,), jnp.int32)],
        [VMEM, VMEM, VMEM, VMEM, SMEM],
        "quarter0",
        out_specs=[VMEM, VMEM, SMEM],
        **cost,
    )(inv, solved_b, *nxt, touched)

    outgoing = call(place_kernel, shape((SUBS, ROWS, TILE), BF), [SMEM] + [VMEM] * 4, "place")(
        touched, t0, r1, r2, r3
    )
    arrived = lax.all_to_all(outgoing, "sub", 0, 0, tiled=True)
    x, leaving = call(
        solve_kernel,
        [shape((2, RHS, TILE), F32), shape((SUBS, RHS, TILE), BF)],
        [SMEM] + [VMEM] * 3,
        "solve",
        scratch=[pltpu.VMEM((2, ROWS, TILE), F32), pltpu.VMEM((2, RHS, TILE), BF)],
    )(reads, arrived, interface_blocks, interface_rhs)
    returned = lax.all_to_all(leaving, "sub", 0, 0, tiled=True)
    x0 = call(pick_kernel, shape((Q, RHS, TILE), BF), [SMEM, VMEM], "pick")(touched, returned)
    x1, x2, x3 = (shift_grp(x0, d) for d in (1, 2, 3))
    wide = pltpu.VMEM((RHS, COLS), BF)
    work = dict(flops=2 * RHS * QUARTER * COLS, nbytes=1 << 20)
    begun = call(own_kernel, shape((RHS, QUARTER), F32), [VMEM] * 3, "interior_own", scratch=[wide], **work)(
        x0, im0, solved_f
    )
    interior = call(final_kernel, shape((RHS, QUARTER), BF), [VMEM] * 7, "interior", scratch=[wide] * 3, **work)(
        begun, im1, im2, im3, x1, x3, x2
    )
    return (interior[None], x)


def solution(mesh):
    in_specs = (
        P("sub", "grp", None),
        P("sub", None, None),
        P("sub", None, None, "grp"),
        P("sub", None, None),
        P(("sub", "grp"), None, None),
        P(("sub", "grp"), None, None),
        P(),
    )
    out_specs = (P("sub", None, "grp"), P(("sub", "grp"), None, None))
    return jax.shard_map(shards, mesh=mesh, in_specs=in_specs, out_specs=out_specs, check_vma=False)
```

```python
import functools

import jax
import jax.numpy as jnp
from jax import lax
from jax.experimental import pallas as pl
from jax.experimental.pallas import tpu as pltpu
from jax.sharding import PartitionSpec as P

JAC = 4
BF = jnp.bfloat16
F32 = jnp.float32
VMEM = pl.BlockSpec(memory_space=pltpu.VMEM)
SMEM = pl.BlockSpec(memory_space=pltpu.SMEM)
HBM = pl.BlockSpec(memory_space=pltpu.HBM)

SUBS = 32
N_INT, QUARTER, TILE, RHS, Q = 2048, 512, 128, 64, 8
COLS = Q * TILE
ROWS = TILE + RHS
HALF = ROWS // 2
PARTS, DEPTH = 4, 512
STREAMS = 8


def dot(a, b, **kw):
    return jnp.dot(a, b, preferred_element_type=F32, **kw)


def dot_nt(a, b):
    return lax.dot_general(a, b, (((1,), (1,)), ((), ())), preferred_element_type=F32)


def shift_grp(x, by):
    return lax.ppermute(x, "grp", [(s, (s + by) % 4) for s in range(4)])


def call(kernel, out_shape, in_specs, name, out_specs=None, scratch=(), flops=0, nbytes=0, mib=8):
    if out_specs is None:
        out_specs = jax.tree.map(lambda _: VMEM, out_shape)
    return pl.pallas_call(
        kernel,
        out_shape=out_shape,
        in_specs=in_specs,
        out_specs=out_specs,
        scratch_shapes=scratch,
        compiler_params=pltpu.CompilerParams(vmem_limit_bytes=mib << 20),
        cost_estimate=pl.CostEstimate(flops=flops, bytes_accessed=nbytes, transcendentals=0),
        name=name,
    )


def block_copies(rel, right, left, cur, left_buf, sem):
    q = lax.rem(lax.axis_index("grp") + rel, 4)
    cols = pl.ds(pl.multiple_of(q * COLS, COLS), COLS)
    copies = []
    for k in range(STREAMS):
        rows = pl.ds(k * (N_INT // STREAMS), N_INT // STREAMS)
        copies.append(pltpu.make_async_copy(right.at[rows, cols], cur.at[rows], sem.at[k]))
    for k in range(2):
        tiles = pl.ds(k * (Q // 2), Q // 2)
        src = left.at[pl.ds(q * Q + k * (Q // 2), Q // 2)]
        copies.append(pltpu.make_async_copy(src, left_buf.at[tiles], sem.at[STREAMS + k]))
    return copies


def make_images(inv, cur, images):
    @pl.loop(0, 2)
    def _(h):
        rows = pl.ds(pl.multiple_of(h * (QUARTER // 2), QUARTER // 2), QUARTER // 2)
        images[rows, :] = dot(inv[rows, :], cur[...]).astype(BF)


def make_tiles(solved, left, images, tiles):
    load = dot_nt(solved, left[...].reshape(COLS, QUARTER))
    for t in range(Q):
        cols = slice(t * TILE, (t + 1) * TILE)
        tiles[t, :TILE] = dot(left[t], images[:, cols]).astype(BF)
        tiles[t, TILE:] = load[:, cols].astype(BF)


def first_kernel(
    inv_h, right, left, forcing_h, tiles, images, solved_f, solved_b, inv, nxt, nxt_left,
    forcing, cur, left_buf, acc, sem, part_sem,
):
    q = lax.rem(lax.axis_index("grp") + 2, 4)
    cols = pl.ds(pl.multiple_of(q * COLS, COLS), COLS)
    parts = []
    for k in range(PARTS):
        rows = pl.ds(k * DEPTH, DEPTH)
        parts.append((
            pltpu.make_async_copy(inv_h.at[:, rows], inv.at[:, rows], part_sem.at[2 * k]),
            pltpu.make_async_copy(right.at[rows, cols], cur.at[rows], part_sem.at[2 * k + 1]),
        ))
        for c in parts[-1]:
            c.start()
    late = [
        pltpu.make_async_copy(forcing_h, forcing, part_sem.at[2 * PARTS]),
        pltpu.make_async_copy(left.at[pl.ds(q * Q, Q)], left_buf, part_sem.at[2 * PARTS + 1]),
    ]
    for c in late:
        c.start()
    following = block_copies(1, right, left, nxt, nxt_left, sem)
    for k in range(PARTS):
        for c in parts[k]:
            c.wait()
        if k == PARTS - 2:
            for c in following:
                c.start()
        part = slice(k * DEPTH, (k + 1) * DEPTH)
        p = dot(inv[:, part], cur[part])
        if k == 0:
            acc[...] = p
        elif k < PARTS - 1:
            acc[...] += p
        else:
            images[...] = (acc[...] + p).astype(BF)
    for c in late:
        c.wait()
    s = dot_nt(forcing[...], inv[...])
    solved_f[...] = s
    solved_b[...] = s.astype(BF)
    make_tiles(solved_b[...], left_buf, images, tiles)
    for c in following:
        c.wait()


def middle_kernel(rel, inv, right, left, solved, cur, cur_left, tiles, images, nxt, nxt_left, sem):
    following = block_copies(rel, right, left, nxt, nxt_left, sem)
    for c in following:
        c.start()
    make_images(inv, cur, images)
    make_tiles(solved[...], cur_left, images, tiles)
    for c in following:
        c.wait()


def last_kernel(inv, solved, cur, cur_left, touched, tiles, images, reads):
    make_images(inv, cur, images)
    make_tiles(solved[...], cur_left, images, tiles)
    sub, g = lax.axis_index("sub"), lax.axis_index("grp")
    first = (sub * 4 + g) * 2

    @pl.loop(0, SUBS)
    def _(s):
        found = jnp.int32(0)
        for k in range(Q):
            tile = touched[s, g * Q + k]
            found = jnp.where((tile >> 1) == (first >> 1), 1 + (tile & 1), found)
        reads[s] = found


def place_kernel(touched, own, r1, r2, r3, out):
    sub, g = lax.axis_index("sub"), lax.axis_index("grp")
    for t in range(Q):
        s = (own[t].astype(F32) + r1[t].astype(F32)) + (r2[t].astype(F32) + r3[t].astype(F32))
        out[touched[sub, g * Q + t] >> 3] = s.astype(BF)


def solve_kernel(reads, arrived, blocks, rhs, x_out, out, total, rounded):
    total[...] = jnp.zeros_like(total)

    @pl.loop(0, SUBS)
    def _(s):
        which = reads[s]

        @pl.when(which > 0)
        def _():
            total[which - 1] += arrived[s].astype(F32)

    row = lax.broadcasted_iota(jnp.int32, (TILE, TILE), 0)
    col = lax.broadcasted_iota(jnp.int32, (TILE, TILE), 1)
    systems, targets, pivots, xs = [], [], [], []
    for t in range(2):
        m = blocks[t] - total[t, :TILE]
        systems.append(m.T)
        targets.append(rhs[t] - total[t, TILE:])
        pivots.append(jnp.sum(jnp.where(row == col, m, 0.0), axis=0, keepdims=True))
        xs.append(targets[t] / pivots[t])
    for _ in range(JAC - 1):
        applied = [dot(xs[t], systems[t], precision=lax.Precision.HIGHEST) for t in range(2)]
        xs = [xs[t] + (targets[t] - applied[t]) / pivots[t] for t in range(2)]
    for t in range(2):
        x_out[t] = xs[t]
        rounded[t] = xs[t].astype(BF)

    @pl.loop(0, SUBS)
    def _(s):
        out[s] = rounded[jnp.maximum(reads[s] - 1, 0)]


def pick_kernel(touched, returned, out):
    sub, g = lax.axis_index("sub"), lax.axis_index("grp")
    for q in range(Q):
        out[q] = returned[touched[sub, g * Q + q] >> 3]


def coupled(tiles, images, wide):
    for q in range(Q):
        wide[:, q * TILE : (q + 1) * TILE] = tiles[q]
    return dot_nt(wide[...], images[...])


def own_kernel(x0, i0, solved, solution_in, out, solution_out, wide):
    out[...] = solved[...] - coupled(x0, i0, wide)
    solution_out[...] = solution_in[...]


def far_kernel(x2, i2, begun, out, wide):
    out[...] = begun[...] - coupled(x2, i2, wide)


def final_kernel(begun, i1, i3, x1, x3, out, *wide):
    acc = begun[...]
    for xr, im, w in zip((x1, x3), (i3, i1), wide):
        acc = acc - coupled(xr, im, w)
    out[...] = acc.astype(BF)


def shards(
    inverse_blocks,
    coupling_right,
    coupling_left,
    interior_rhs,
    interface_blocks,
    interface_rhs,
    touched,
):
    shape = jax.ShapeDtypeStruct
    inverse, right, left, forcing = inverse_blocks[0], coupling_right[0], coupling_left[0], interior_rhs[0]
    tiles, images = shape((Q, ROWS, TILE), BF), shape((QUARTER, COLS), BF)
    block = [shape((N_INT, COLS), BF), shape((Q, TILE, QUARTER), BF)]
    dma = pltpu.SemaphoreType.DMA
    cost = dict(flops=2 * QUARTER * N_INT * COLS, nbytes=N_INT * COLS * 2, mib=20)
    inverse, right, left, forcing = (
        pltpu.with_memory_space_constraint(v, pltpu.HBM) for v in (inverse, right, left, forcing)
    )
    t2, im2, solved_f, solved_b, inv, *nxt = call(
        first_kernel,
        [tiles, images, shape((RHS, QUARTER), F32), shape((RHS, QUARTER), BF), shape((QUARTER, N_INT), BF)] + block,
        [HBM] * 4,
        "quarter2",
        scratch=[
            pltpu.VMEM((RHS, N_INT), BF),
            pltpu.VMEM((N_INT, COLS), BF),
            pltpu.VMEM((Q, TILE, QUARTER), BF),
            pltpu.VMEM((QUARTER, COLS), F32),
            dma((STREAMS + 2,)),
            dma((2 * PARTS + 2,)),
        ],
        **cost,
    )(inverse, right, left, forcing)
    r2 = shift_grp(t2, 2)
    middle = lambda rel, following: call(
        functools.partial(middle_kernel, following),
        [tiles, images] + block,
        [VMEM, HBM, HBM, VMEM, VMEM, VMEM],
        f"quarter{rel}",
        scratch=[dma((STREAMS + 2,))],
        **cost,
    )
    t1, im1, *nxt = middle(1, 3)(inv, right, left, solved_b, *nxt)
    r1 = shift_grp(t1, 1)
    t3, im3, *nxt = middle(3, 0)(inv, right, left, solved_b, *nxt)
    r3 = shift_grp(t3, 3)
    t0, im0, reads = call(
        last_kernel,
        [tiles, images, shape((SUBS,), jnp.int32)],
        [VMEM, VMEM, VMEM, VMEM, SMEM],
        "quarter0",
        out_specs=[VMEM, VMEM, SMEM],
        **cost,
    )(inv, solved_b, *nxt, touched)

    outgoing = call(place_kernel, shape((SUBS, ROWS, TILE), BF), [SMEM] + [VMEM] * 4, "place")(
        touched, t0, r1, r2, r3
    )
    arrived = lax.all_to_all(outgoing, "sub", 0, 0, tiled=True)
    x, leaving = call(
        solve_kernel,
        [shape((2, RHS, TILE), F32), shape((SUBS, RHS, TILE), BF)],
        [SMEM] + [VMEM] * 3,
        "solve",
        scratch=[pltpu.VMEM((2, ROWS, TILE), F32), pltpu.VMEM((2, RHS, TILE), BF)],
    )(reads, arrived, interface_blocks, interface_rhs)
    returned = lax.all_to_all(leaving, "sub", 0, 0, tiled=True)
    x0 = call(pick_kernel, shape((Q, RHS, TILE), BF), [SMEM, VMEM], "pick")(touched, returned)
    x1, x2, x3 = (shift_grp(x0, d) for d in (1, 2, 3))
    wide = pltpu.VMEM((RHS, COLS), BF)
    work = dict(flops=2 * RHS * QUARTER * COLS, nbytes=1 << 20)
    so_far = shape((RHS, QUARTER), F32)
    begun, x = call(own_kernel, [so_far, shape(x.shape, F32)], [VMEM] * 4, "interior_own", scratch=[wide], **work)(
        x0, im0, solved_f, x
    )
    begun = call(far_kernel, so_far, [VMEM] * 3, "interior_far", scratch=[wide], **work)(x2, im2, begun)
    interior = call(final_kernel, shape((RHS, QUARTER), BF), [VMEM] * 5, "interior", scratch=[wide] * 2, **work)(
        begun, im1, im3, x1, x3
    )
    return (interior[None], x)


def solution(mesh):
    in_specs = (
        P("sub", "grp", None),
        P("sub", None, None),
        P("sub", None, None, "grp"),
        P("sub", None, None),
        P(("sub", "grp"), None, None),
        P(("sub", "grp"), None, None),
        P(),
    )
    out_specs = (P("sub", None, "grp"), P(("sub", "grp"), None, None))
    return jax.shard_map(shards, mesh=mesh, in_specs=in_specs, out_specs=out_specs, check_vma=False)
```

```python
import functools

import jax
import jax.numpy as jnp
from jax import lax
from jax.experimental import pallas as pl
from jax.experimental.pallas import tpu as pltpu
from jax.sharding import PartitionSpec as P

JAC = 4
BF = jnp.bfloat16
F32 = jnp.float32
VMEM = pl.BlockSpec(memory_space=pltpu.VMEM)
SMEM = pl.BlockSpec(memory_space=pltpu.SMEM)
HBM = pl.BlockSpec(memory_space=pltpu.HBM)

SUBS = 32
N_INT, QUARTER, TILE, RHS, Q = 2048, 512, 128, 64, 8
COLS = Q * TILE
ROWS = TILE + RHS
HALF = ROWS // 2
PARTS, DEPTH = 4, 512
STREAMS = 8


def dot(a, b, **kw):
    return jnp.dot(a, b, preferred_element_type=F32, **kw)


def dot_nt(a, b):
    return lax.dot_general(a, b, (((1,), (1,)), ((), ())), preferred_element_type=F32)


def shift_grp(x, by):
    return lax.ppermute(x, "grp", [(s, (s + by) % 4) for s in range(4)])


def call(kernel, out_shape, in_specs, name, out_specs=None, scratch=(), flops=0, nbytes=0, mib=8):
    if out_specs is None:
        out_specs = jax.tree.map(lambda _: VMEM, out_shape)
    return pl.pallas_call(
        kernel,
        out_shape=out_shape,
        in_specs=in_specs,
        out_specs=out_specs,
        scratch_shapes=scratch,
        compiler_params=pltpu.CompilerParams(vmem_limit_bytes=mib << 20),
        cost_estimate=pl.CostEstimate(flops=flops, bytes_accessed=nbytes, transcendentals=0),
        name=name,
    )


def block_copies(rel, right, left, cur, left_buf, sem):
    q = lax.rem(lax.axis_index("grp") + rel, 4)
    cols = pl.ds(pl.multiple_of(q * COLS, COLS), COLS)
    copies = []
    for k in range(STREAMS):
        rows = pl.ds(k * (N_INT // STREAMS), N_INT // STREAMS)
        copies.append(pltpu.make_async_copy(right.at[rows, cols], cur.at[rows], sem.at[k]))
    for k in range(2):
        tiles = pl.ds(k * (Q // 2), Q // 2)
        src = left.at[pl.ds(q * Q + k * (Q // 2), Q // 2)]
        copies.append(pltpu.make_async_copy(src, left_buf.at[tiles], sem.at[STREAMS + k]))
    return copies


def make_images(inv, cur, images):
    @pl.loop(0, 2)
    def _(h):
        rows = pl.ds(pl.multiple_of(h * (QUARTER // 2), QUARTER // 2), QUARTER // 2)
        images[rows, :] = dot(inv[rows, :], cur[...]).astype(BF)


def make_tiles(solved, left, images, tiles):
    load = dot_nt(solved, left[...].reshape(COLS, QUARTER))
    for t in range(Q):
        cols = slice(t * TILE, (t + 1) * TILE)
        tiles[t, :TILE] = dot(left[t], images[:, cols]).astype(BF)
        tiles[t, TILE:] = load[:, cols].astype(BF)


def first_kernel(
    inv_h, right, left, forcing_h, tiles, images, solved_f, solved_b, inv, nxt, nxt_left,
    forcing, cur, left_buf, acc, sem, part_sem,
):
    q = lax.rem(lax.axis_index("grp") + 2, 4)
    cols = pl.ds(pl.multiple_of(q * COLS, COLS), COLS)
    parts = []
    for k in range(PARTS):
        rows = pl.ds(k * DEPTH, DEPTH)
        parts.append((
            pltpu.make_async_copy(inv_h.at[:, rows], inv.at[:, rows], part_sem.at[2 * k]),
            pltpu.make_async_copy(right.at[rows, cols], cur.at[rows], part_sem.at[2 * k + 1]),
        ))
        for c in parts[-1]:
            c.start()
    late = [
        pltpu.make_async_copy(forcing_h, forcing, part_sem.at[2 * PARTS]),
        pltpu.make_async_copy(left.at[pl.ds(q * Q, Q)], left_buf, part_sem.at[2 * PARTS + 1]),
    ]
    for c in late:
        c.start()
    following = block_copies(1, right, left, nxt, nxt_left, sem)
    for k in range(PARTS):
        for c in parts[k]:
            c.wait()
        if k == PARTS - 2:
            for c in following:
                c.start()
        part = slice(k * DEPTH, (k + 1) * DEPTH)
        p = dot(inv[:, part], cur[part])
        if k == 0:
            acc[...] = p
        elif k < PARTS - 1:
            acc[...] += p
        else:
            images[...] = (acc[...] + p).astype(BF)
    for c in late:
        c.wait()
    s = dot_nt(forcing[...], inv[...])
    solved_f[...] = s
    solved_b[...] = s.astype(BF)
    make_tiles(solved_b[...], left_buf, images, tiles)
    for c in following:
        c.wait()


def middle_kernel(rel, inv, right, left, solved, cur, cur_left, tiles, images, nxt, nxt_left, sem):
    following = block_copies(rel, right, left, nxt, nxt_left, sem)
    for c in following:
        c.start()
    make_images(inv, cur, images)
    make_tiles(solved[...], cur_left, images, tiles)
    for c in following:
        c.wait()


def last_kernel(inv, solved, cur, cur_left, touched, tiles, images, readers, owners):
    make_images(inv, cur, images)
    make_tiles(solved[...], cur_left, images, tiles)
    sub, g = lax.axis_index("sub"), lax.axis_index("grp")
    for k in range(Q):
        owners[k] = touched[sub, g * Q + k] >> 3
    dev = sub * 4 + g
    readers[2 * SUBS] = 0
    readers[2 * SUBS + 1] = 0

    @pl.loop(0, SUBS)
    def _(s):
        found = jnp.int32(-1)
        for k in range(Q):
            tile = touched[s, g * Q + k]
            found = jnp.where((tile >> 1) == dev, tile & 1, found)

        @pl.when(found >= 0)
        def _():
            n = readers[2 * SUBS + found]
            readers[SUBS * found + n] = s
            readers[2 * SUBS + found] = n + 1


def place_kernel(owners, own, r1, r2, r3, out):
    for t in range(Q):
        s = (own[t].astype(F32) + r1[t].astype(F32)) + (r2[t].astype(F32) + r3[t].astype(F32))
        out[owners[t]] = s.astype(BF)


def solve_kernel(readers, arrived, blocks, rhs, x_out, out):
    totals = [
        lax.fori_loop(
            0,
            readers[2 * SUBS + t],
            lambda j, acc: acc + arrived[readers[SUBS * t + j]].astype(F32),
            jnp.zeros((ROWS, TILE), F32),
        )
        for t in range(2)
    ]
    row = lax.broadcasted_iota(jnp.int32, (TILE, TILE), 0)
    col = lax.broadcasted_iota(jnp.int32, (TILE, TILE), 1)
    systems, targets, pivots, xs = [], [], [], []
    for t in range(2):
        m = blocks[t] - totals[t][:TILE]
        systems.append(m.T)
        targets.append(rhs[t] - totals[t][TILE:])
        pivots.append(jnp.sum(jnp.where(row == col, m, 0.0), axis=0, keepdims=True))
        xs.append(targets[t] / pivots[t])
    for _ in range(JAC - 1):
        applied = [dot(xs[t], systems[t], precision=lax.Precision.HIGHEST) for t in range(2)]
        xs = [xs[t] + (targets[t] - applied[t]) / pivots[t] for t in range(2)]
    for t in range(2):
        x_out[t] = xs[t]
        rounded = xs[t].astype(BF)

        @pl.loop(0, readers[2 * SUBS + t])
        def _(j):
            out[readers[SUBS * t + j]] = rounded


def pick_kernel(owners, returned, out):
    for q in range(Q):
        out[q] = returned[owners[q]]


def coupled(tiles, images, wide):
    for q in range(Q):
        wide[:, q * TILE : (q + 1) * TILE] = tiles[q]
    return dot_nt(wide[...], images[...])


def own_kernel(x0, i0, solved, solution_in, out, solution_out, wide):
    out[...] = solved[...] - coupled(x0, i0, wide)
    solution_out[...] = solution_in[...]


def far_kernel(x2, i2, begun, out, wide):
    out[...] = begun[...] - coupled(x2, i2, wide)


def final_kernel(begun, i1, i3, x1, x3, out, *wide):
    acc = begun[...]
    for xr, im, w in zip((x1, x3), (i3, i1), wide):
        acc = acc - coupled(xr, im, w)
    out[...] = acc.astype(BF)


def shards(
    inverse_blocks,
    coupling_right,
    coupling_left,
    interior_rhs,
    interface_blocks,
    interface_rhs,
    touched,
):
    shape = jax.ShapeDtypeStruct
    inverse, right, left, forcing = inverse_blocks[0], coupling_right[0], coupling_left[0], interior_rhs[0]
    tiles, images = shape((Q, ROWS, TILE), BF), shape((QUARTER, COLS), BF)
    block = [shape((N_INT, COLS), BF), shape((Q, TILE, QUARTER), BF)]
    dma = pltpu.SemaphoreType.DMA
    cost = dict(flops=2 * QUARTER * N_INT * COLS, nbytes=N_INT * COLS * 2, mib=20)
    inverse, right, left, forcing = (
        pltpu.with_memory_space_constraint(v, pltpu.HBM) for v in (inverse, right, left, forcing)
    )
    t2, im2, solved_f, solved_b, inv, *nxt = call(
        first_kernel,
        [tiles, images, shape((RHS, QUARTER), F32), shape((RHS, QUARTER), BF), shape((QUARTER, N_INT), BF)] + block,
        [HBM] * 4,
        "quarter2",
        scratch=[
            pltpu.VMEM((RHS, N_INT), BF),
            pltpu.VMEM((N_INT, COLS), BF),
            pltpu.VMEM((Q, TILE, QUARTER), BF),
            pltpu.VMEM((QUARTER, COLS), F32),
            dma((STREAMS + 2,)),
            dma((2 * PARTS + 2,)),
        ],
        **cost,
    )(inverse, right, left, forcing)
    r2 = shift_grp(t2, 2)
    middle = lambda rel, following: call(
        functools.partial(middle_kernel, following),
        [tiles, images] + block,
        [VMEM, HBM, HBM, VMEM, VMEM, VMEM],
        f"quarter{rel}",
        scratch=[dma((STREAMS + 2,))],
        **cost,
    )
    t1, im1, *nxt = middle(1, 3)(inv, right, left, solved_b, *nxt)
    r1 = shift_grp(t1, 1)
    t3, im3, *nxt = middle(3, 0)(inv, right, left, solved_b, *nxt)
    r3 = shift_grp(t3, 3)
    t0, im0, readers, owners = call(
        last_kernel,
        [tiles, images, shape((2 * SUBS + 2,), jnp.int32), shape((Q,), jnp.int32)],
        [VMEM, VMEM, VMEM, VMEM, SMEM],
        "quarter0",
        out_specs=[VMEM, VMEM, SMEM, SMEM],
        **cost,
    )(inv, solved_b, *nxt, touched)

    outgoing = call(place_kernel, shape((SUBS, ROWS, TILE), BF), [SMEM] + [VMEM] * 4, "place")(
        owners, t0, r1, r2, r3
    )
    arrived = lax.all_to_all(outgoing, "sub", 0, 0, tiled=True)
    x, leaving = call(
        solve_kernel,
        [shape((2, RHS, TILE), F32), shape((SUBS, RHS, TILE), BF)],
        [SMEM] + [VMEM] * 3,
        "solve",
    )(readers, arrived, interface_blocks, interface_rhs)
    returned = lax.all_to_all(leaving, "sub", 0, 0, tiled=True)
    x0 = call(pick_kernel, shape((Q, RHS, TILE), BF), [SMEM, VMEM], "pick")(owners, returned)
    x1, x2, x3 = (shift_grp(x0, d) for d in (1, 2, 3))
    wide = pltpu.VMEM((RHS, COLS), BF)
    work = dict(flops=2 * RHS * QUARTER * COLS, nbytes=1 << 20)
    so_far = shape((RHS, QUARTER), F32)
    begun, x = call(own_kernel, [so_far, shape(x.shape, F32)], [VMEM] * 4, "interior_own", scratch=[wide], **work)(
        x0, im0, solved_f, x
    )
    begun = call(far_kernel, so_far, [VMEM] * 3, "interior_far", scratch=[wide], **work)(x2, im2, begun)
    interior = call(final_kernel, shape((RHS, QUARTER), BF), [VMEM] * 5, "interior", scratch=[wide] * 2, **work)(
        begun, im1, im3, x1, x3
    )
    return (interior[None], x)


def solution(mesh):
    in_specs = (
        P("sub", "grp", None),
        P("sub", None, None),
        P("sub", None, None, "grp"),
        P("sub", None, None),
        P(("sub", "grp"), None, None),
        P(("sub", "grp"), None, None),
        P(),
    )
    out_specs = (P("sub", None, "grp"), P(("sub", "grp"), None, None))
    return jax.shard_map(shards, mesh=mesh, in_specs=in_specs, out_specs=out_specs, check_vma=False)
```

```python
import functools

import jax
import jax.numpy as jnp
from jax import lax
from jax.experimental import pallas as pl
from jax.experimental.pallas import tpu as pltpu
from jax.sharding import PartitionSpec as P

JAC = 4
BF = jnp.bfloat16
F32 = jnp.float32
VMEM = pl.BlockSpec(memory_space=pltpu.VMEM)
SMEM = pl.BlockSpec(memory_space=pltpu.SMEM)
HBM = pl.BlockSpec(memory_space=pltpu.HBM)

SUBS = 32
N_INT, QUARTER, TILE, RHS, Q = 2048, 512, 128, 64, 8
COLS = Q * TILE
ROWS = TILE + RHS
HALF = ROWS // 2
PARTS, DEPTH = 4, 512
STREAMS = 8


def dot(a, b, **kw):
    return jnp.dot(a, b, preferred_element_type=F32, **kw)


def dot_nt(a, b):
    return lax.dot_general(a, b, (((1,), (1,)), ((), ())), preferred_element_type=F32)


def shift_grp(x, by):
    return lax.ppermute(x, "grp", [(s, (s + by) % 4) for s in range(4)])


def call(kernel, out_shape, in_specs, name, out_specs=None, scratch=(), flops=0, nbytes=0, mib=8):
    if out_specs is None:
        out_specs = jax.tree.map(lambda _: VMEM, out_shape)
    return pl.pallas_call(
        kernel,
        out_shape=out_shape,
        in_specs=in_specs,
        out_specs=out_specs,
        scratch_shapes=scratch,
        compiler_params=pltpu.CompilerParams(vmem_limit_bytes=mib << 20),
        cost_estimate=pl.CostEstimate(flops=flops, bytes_accessed=nbytes, transcendentals=0),
        name=name,
    )


def block_copies(rel, right, left, cur, left_buf, sem):
    q = lax.rem(lax.axis_index("grp") + rel, 4)
    cols = pl.ds(pl.multiple_of(q * COLS, COLS), COLS)
    copies = []
    for k in range(STREAMS):
        rows = pl.ds(k * (N_INT // STREAMS), N_INT // STREAMS)
        copies.append(pltpu.make_async_copy(right.at[rows, cols], cur.at[rows], sem.at[k]))
    for k in range(2):
        tiles = pl.ds(k * (Q // 2), Q // 2)
        src = left.at[pl.ds(q * Q + k * (Q // 2), Q // 2)]
        copies.append(pltpu.make_async_copy(src, left_buf.at[tiles], sem.at[STREAMS + k]))
    return copies


def make_images(inv, cur, images):
    @pl.loop(0, 2)
    def _(h):
        rows = pl.ds(pl.multiple_of(h * (QUARTER // 2), QUARTER // 2), QUARTER // 2)
        images[rows, :] = dot(inv[rows, :], cur[...]).astype(BF)


def make_tiles(solved, left, images, tiles):
    load = dot_nt(solved, left[...].reshape(COLS, QUARTER))
    for t in range(Q):
        cols = slice(t * TILE, (t + 1) * TILE)
        tiles[t, :TILE] = dot(left[t], images[:, cols]).astype(BF)
        tiles[t, TILE:] = load[:, cols].astype(BF)


def first_kernel(
    inv_h, right, left, forcing_h, tiles, images, solved_f, solved_b, inv, nxt, nxt_left,
    forcing, cur, left_buf, acc, sem, part_sem,
):
    q = lax.rem(lax.axis_index("grp") + 2, 4)
    cols = pl.ds(pl.multiple_of(q * COLS, COLS), COLS)
    parts = []
    for k in range(PARTS):
        rows = pl.ds(k * DEPTH, DEPTH)
        parts.append((
            pltpu.make_async_copy(inv_h.at[:, rows], inv.at[:, rows], part_sem.at[2 * k]),
            pltpu.make_async_copy(right.at[rows, cols], cur.at[rows], part_sem.at[2 * k + 1]),
        ))
        for c in parts[-1]:
            c.start()
    late = [
        pltpu.make_async_copy(forcing_h, forcing, part_sem.at[2 * PARTS]),
        pltpu.make_async_copy(left.at[pl.ds(q * Q, Q)], left_buf, part_sem.at[2 * PARTS + 1]),
    ]
    for c in late:
        c.start()
    following = block_copies(1, right, left, nxt, nxt_left, sem)
    for k in range(PARTS):
        for c in parts[k]:
            c.wait()
        if k == PARTS - 2:
            for c in following:
                c.start()
        part = slice(k * DEPTH, (k + 1) * DEPTH)
        p = dot(inv[:, part], cur[part])
        if k == 0:
            acc[...] = p
        elif k < PARTS - 1:
            acc[...] += p
        else:
            images[...] = (acc[...] + p).astype(BF)
    for c in late:
        c.wait()
    s = dot_nt(forcing[...], inv[...])
    solved_f[...] = s
    solved_b[...] = s.astype(BF)
    make_tiles(solved_b[...], left_buf, images, tiles)
    for c in following:
        c.wait()


def middle_kernel(rel, inv, right, left, solved, cur, cur_left, tiles, images, nxt, nxt_left, sem):
    following = block_copies(rel, right, left, nxt, nxt_left, sem)
    for c in following:
        c.start()
    make_images(inv, cur, images)
    make_tiles(solved[...], cur_left, images, tiles)
    for c in following:
        c.wait()


def last_kernel(inv, solved, cur, cur_left, touched, tiles, images, readers, owners):
    make_images(inv, cur, images)
    make_tiles(solved[...], cur_left, images, tiles)
    sub, g = lax.axis_index("sub"), lax.axis_index("grp")
    for k in range(Q):
        owners[k] = touched[sub, g * Q + k] >> 3
    dev = sub * 4 + g
    readers[2 * SUBS] = 0
    readers[2 * SUBS + 1] = 0

    @pl.loop(0, SUBS)
    def _(s):
        found = jnp.int32(-1)
        for k in range(Q):
            tile = touched[s, g * Q + k]
            found = jnp.where((tile >> 1) == dev, tile & 1, found)

        @pl.when(found >= 0)
        def _():
            n = readers[2 * SUBS + found]
            readers[SUBS * found + n] = s
            readers[2 * SUBS + found] = n + 1


def place_kernel(owners, own, r1, r2, r3, out):
    for t in range(Q):
        s = (own[t].astype(F32) + r1[t].astype(F32)) + (r2[t].astype(F32) + r3[t].astype(F32))
        out[owners[t]] = s.astype(BF)


def solve_kernel(readers, arrived, blocks, rhs, x_out, out):
    def arrival(t, j):
        return arrived[readers[SUBS * t + j]].astype(F32)

    totals = []
    for t in range(2):
        count = readers[2 * SUBS + t]
        fours = count >> 2
        total = lax.fori_loop(
            0,
            fours,
            lambda j, acc: acc
            + (
                (arrival(t, 4 * j) + arrival(t, 4 * j + 1))
                + (arrival(t, 4 * j + 2) + arrival(t, 4 * j + 3))
            ),
            jnp.zeros((ROWS, TILE), F32),
        )
        totals.append(lax.fori_loop(4 * fours, count, lambda j, acc: acc + arrival(t, j), total))
    row = lax.broadcasted_iota(jnp.int32, (TILE, TILE), 0)
    col = lax.broadcasted_iota(jnp.int32, (TILE, TILE), 1)
    systems, targets, pivots, xs = [], [], [], []
    for t in range(2):
        m = blocks[t] - totals[t][:TILE]
        systems.append(m.T)
        targets.append(rhs[t] - totals[t][TILE:])
        pivots.append(jnp.sum(jnp.where(row == col, m, 0.0), axis=0, keepdims=True))
        xs.append(targets[t] / pivots[t])
    for _ in range(JAC - 1):
        applied = [dot(xs[t], systems[t], precision=lax.Precision.HIGHEST) for t in range(2)]
        xs = [xs[t] + (targets[t] - applied[t]) / pivots[t] for t in range(2)]
    for t in range(2):
        x_out[t] = xs[t]
        rounded = xs[t].astype(BF)

        @pl.loop(0, readers[2 * SUBS + t])
        def _(j):
            out[readers[SUBS * t + j]] = rounded


def pick_kernel(owners, returned, out):
    for q in range(Q):
        out[q] = returned[owners[q]]


def coupled(tiles, images, wide):
    for q in range(Q):
        wide[:, q * TILE : (q + 1) * TILE] = tiles[q]
    return dot_nt(wide[...], images[...])


def own_kernel(x0, i0, solved, solution_in, out, solution_out, wide):
    out[...] = solved[...] - coupled(x0, i0, wide)
    solution_out[...] = solution_in[...]


def far_kernel(x2, i2, begun, out, wide):
    out[...] = begun[...] - coupled(x2, i2, wide)


def final_kernel(begun, i1, i3, x1, x3, out, *wide):
    acc = begun[...]
    for xr, im, w in zip((x1, x3), (i3, i1), wide):
        acc = acc - coupled(xr, im, w)
    out[...] = acc.astype(BF)


def shards(
    inverse_blocks,
    coupling_right,
    coupling_left,
    interior_rhs,
    interface_blocks,
    interface_rhs,
    touched,
):
    shape = jax.ShapeDtypeStruct
    inverse, right, left, forcing = inverse_blocks[0], coupling_right[0], coupling_left[0], interior_rhs[0]
    tiles, images = shape((Q, ROWS, TILE), BF), shape((QUARTER, COLS), BF)
    block = [shape((N_INT, COLS), BF), shape((Q, TILE, QUARTER), BF)]
    dma = pltpu.SemaphoreType.DMA
    cost = dict(flops=2 * QUARTER * N_INT * COLS, nbytes=N_INT * COLS * 2, mib=20)
    inverse, right, left, forcing = (
        pltpu.with_memory_space_constraint(v, pltpu.HBM) for v in (inverse, right, left, forcing)
    )
    t2, im2, solved_f, solved_b, inv, *nxt = call(
        first_kernel,
        [tiles, images, shape((RHS, QUARTER), F32), shape((RHS, QUARTER), BF), shape((QUARTER, N_INT), BF)] + block,
        [HBM] * 4,
        "quarter2",
        scratch=[
            pltpu.VMEM((RHS, N_INT), BF),
            pltpu.VMEM((N_INT, COLS), BF),
            pltpu.VMEM((Q, TILE, QUARTER), BF),
            pltpu.VMEM((QUARTER, COLS), F32),
            dma((STREAMS + 2,)),
            dma((2 * PARTS + 2,)),
        ],
        **cost,
    )(inverse, right, left, forcing)
    r2 = shift_grp(t2, 2)
    middle = lambda rel, following: call(
        functools.partial(middle_kernel, following),
        [tiles, images] + block,
        [VMEM, HBM, HBM, VMEM, VMEM, VMEM],
        f"quarter{rel}",
        scratch=[dma((STREAMS + 2,))],
        **cost,
    )
    t1, im1, *nxt = middle(1, 3)(inv, right, left, solved_b, *nxt)
    r1 = shift_grp(t1, 1)
    t3, im3, *nxt = middle(3, 0)(inv, right, left, solved_b, *nxt)
    r3 = shift_grp(t3, 3)
    t0, im0, readers, owners = call(
        last_kernel,
        [tiles, images, shape((2 * SUBS + 2,), jnp.int32), shape((Q,), jnp.int32)],
        [VMEM, VMEM, VMEM, VMEM, SMEM],
        "quarter0",
        out_specs=[VMEM, VMEM, SMEM, SMEM],
        **cost,
    )(inv, solved_b, *nxt, touched)

    outgoing = call(place_kernel, shape((SUBS, ROWS, TILE), BF), [SMEM] + [VMEM] * 4, "place")(
        owners, t0, r1, r2, r3
    )
    arrived = lax.all_to_all(outgoing, "sub", 0, 0, tiled=True)
    x, leaving = call(
        solve_kernel,
        [shape((2, RHS, TILE), F32), shape((SUBS, RHS, TILE), BF)],
        [SMEM] + [VMEM] * 3,
        "solve",
    )(readers, arrived, interface_blocks, interface_rhs)
    returned = lax.all_to_all(leaving, "sub", 0, 0, tiled=True)
    x0 = call(pick_kernel, shape((Q, RHS, TILE), BF), [SMEM, VMEM], "pick")(owners, returned)
    x1, x2, x3 = (shift_grp(x0, d) for d in (1, 2, 3))
    wide = pltpu.VMEM((RHS, COLS), BF)
    work = dict(flops=2 * RHS * QUARTER * COLS, nbytes=1 << 20)
    so_far = shape((RHS, QUARTER), F32)
    begun, x = call(own_kernel, [so_far, shape(x.shape, F32)], [VMEM] * 4, "interior_own", scratch=[wide], **work)(
        x0, im0, solved_f, x
    )
    begun = call(far_kernel, so_far, [VMEM] * 3, "interior_far", scratch=[wide], **work)(x2, im2, begun)
    interior = call(final_kernel, shape((RHS, QUARTER), BF), [VMEM] * 5, "interior", scratch=[wide] * 2, **work)(
        begun, im1, im3, x1, x3
    )
    return (interior[None], x)


def solution(mesh):
    in_specs = (
        P("sub", "grp", None),
        P("sub", None, None),
        P("sub", None, None, "grp"),
        P("sub", None, None),
        P(("sub", "grp"), None, None),
        P(("sub", "grp"), None, None),
        P(),
    )
    out_specs = (P("sub", None, "grp"), P(("sub", "grp"), None, None))
    return jax.shard_map(shards, mesh=mesh, in_specs=in_specs, out_specs=out_specs, check_vma=False)
```
